32 devices in a mesh: feat: 16 (over z, y, core), width: 2 (over x).
Axes of the slice: x: 2, y: 2, z: 4, core: 2. Of those that a mesh axis runs over, the one named last changes fastest.
Arguments:
- dec_rows: bfloat16 [32768, 8192], P('feat', 'width'), may hold values from -6 to 6
- enc_rows: bfloat16 [32768, 8192], P('feat', 'width'), may hold values from -0.0625 to 0.0625
- src_act: float32 [4096], replicated, may hold values from 0.25 to 4
- src_slots: int32 [256, 12], P('feat'), may hold values from 0 to 15, as said below
- counts: int32 [256], P('feat'), may hold values from 1 to 12, as said below
- used_tiles: int32 [8, 16], replicated, may hold values from 0 to 31, as said below
Outputs:
- edges: bfloat16 [256, 12, 128, 128], P('feat', None, 'width')
The draws below stay inside these ranges and needn't reach their ends.
Inputs may be any that keep to these rules, and one draw needn't show every extreme that they name: `src_slots`: the slot numbers in one row are distinct. Slots 0 to counts - 1 of a row are live; some row has all 12 live. `used_tiles`: each row rises strictly; of each aligned run of 16 tile numbers exactly half are listed.
All inputs are finite; a program needn't handle non-finite values.
Results may differ from the reference program's by a relative error of at most 0.001.
Values may be sent and summed in bfloat16 or wider, within the bound.
A program may use at most 192 MiB of HBM per device.

```python
import math
import jax
import jax.numpy as jnp
from jax import lax

D = 8192
LAYERS = 8
SRC = 4096
TGT = 4096
TILE = 128
MAXS = 12
GROUP = 2
S_TILES = 32
T_TILES = 32
USED = 16


def draw_src_slots(key, part):
    keys = jax.random.split(jax.random.fold_in(key, 11), LAYERS * T_TILES)
    picked = jax.vmap(lambda single: jax.random.permutation(single, USED)[:MAXS])(keys)
    return picked.astype(jnp.int32)


def draw_counts(key, part):
    first, second, third = jax.random.split(jax.random.fold_in(key, 23), 3)
    total = LAYERS * T_TILES
    heavy = jax.random.randint(first, (total,), 0, 4)
    light = jax.random.randint(second, (total,), 1, MAXS // 2 + 1)
    values = jnp.where(heavy == 0, MAXS, light)
    chosen = jax.random.randint(third, (), 0, total)
    values = values.at[chosen].set(MAXS)
    return values.astype(jnp.int32)


def draw_used_tiles(key, part):
    per_member = S_TILES // GROUP
    take_count = USED // GROUP
    keys = jax.random.split(jax.random.fold_in(key, 37), LAYERS * GROUP)
    picked = jax.vmap(lambda single: jnp.sort(jax.random.permutation(single, per_member)[:take_count]))(keys)
    offsets = jnp.arange(LAYERS * GROUP, dtype=jnp.int32) % GROUP * per_member
    return (picked + offsets[:, None]).reshape(LAYERS, USED).astype(jnp.int32)


def levels(rng, extent, pieces, smallest, largest):
    gain, own = 1.0, jax.random.fold_in(rng, 6)
    for position, parts in pieces:
        steps = jnp.exp(jax.random.uniform(jax.random.fold_in(own, position), (parts,), jnp.float32, smallest / len(pieces), largest / len(pieces)))
        gain = gain * jnp.repeat(steps, extent[position] // parts).reshape([-1 if axis == position else 1 for axis in range(len(extent))])
    return gain


def normal_values(own_key, extent, spread, reach, pieces=(), kind=jnp.bfloat16):
    entries = spread * jax.random.normal(own_key, extent, jnp.float32)
    if pieces:
        entries = entries * levels(own_key, extent, pieces, -0.22, 0.18)
    return jnp.clip(entries, -reach, reach).astype(kind)


def setup_inputs(seed: int = 0) -> dict:
    key_list = jax.random.split(jax.random.key(seed), 7)
    dec_rows = normal_values(key_list[0], (LAYERS * SRC, D), 1.0, 6.0, ((0, 16), (1, 2)))
    enc_rows = normal_values(key_list[1], (LAYERS * TGT, D), D ** -0.5, 0.0625, ((0, 16), (1, 2)))
    src_act = jnp.clip(jnp.exp(jax.random.uniform(key_list[2], (SRC,), jnp.float32, math.log(0.25), math.log(4.0))), 0.25, 4.0)
    src_slots = draw_src_slots(jax.random.fold_in(key_list[6], 71), 0)
    counts = draw_counts(jax.random.fold_in(key_list[6], 71), 0)
    used_tiles = draw_used_tiles(jax.random.fold_in(key_list[6], 71), 0)
    return dict(dec_rows=dec_rows, enc_rows=enc_rows, src_act=src_act, src_slots=src_slots, counts=counts, used_tiles=used_tiles)


def reference(dec_rows, enc_rows, src_act, src_slots, counts, used_tiles):
    source_tiles = SRC // TILE
    target_tiles = TGT // TILE
    dec_tiles = dec_rows.reshape(LAYERS * source_tiles, TILE, D)
    act_tiles = src_act.reshape(source_tiles, TILE)

    def one_tile(index):
        layer_at = index // target_tiles
        tile_at = index % target_tiles
        start = (layer_at * TGT + tile_at * TILE).astype(jnp.int32)
        target = lax.dynamic_slice_in_dim(enc_rows, start, TILE, 0)
        tile_ids = used_tiles[layer_at][src_slots[index]].astype(jnp.int32)
        src_rows = dec_tiles[(layer_at * source_tiles + tile_ids).astype(jnp.int32)].reshape(MAXS * TILE, D)
        products = lax.dot_general(src_rows, target, (((1,), (1,)), ((), ())), preferred_element_type=jnp.float32)
        products = products.reshape(MAXS, TILE, TILE)
        scaled = products * act_tiles[tile_ids][:, :, None]
        is_live = jnp.arange(MAXS, dtype=jnp.int32) < counts[index]
        return jnp.where(is_live[:, None, None], scaled, jnp.zeros_like(scaled)).astype(jnp.bfloat16)

    return lax.map(one_tile, jnp.arange(LAYERS * target_tiles, dtype=jnp.int32))
```

```python
import functools

import jax
import jax.numpy as jnp
from jax import lax
from jax.experimental import pallas as pl
from jax.experimental.pallas import tpu as pltpu
from jax.sharding import PartitionSpec as P

CHUNK = 8
TOP = 32767.0
MESH = pl.DeviceIdType.MESH
DMA = pltpu.SemaphoreType.DMA
PART = 256
RAW = 4


class Plan:
    def __init__(self, steps, wanted, share):
        self.steps = steps
        self.each = min(int(wanted * share) // steps, CHUNK)
        self.rest = -(-(wanted - self.each * steps) // CHUNK)
        self.lead = self.each * steps
        self.slots = self.lead + self.rest * CHUNK
        self.first = steps if self.each else 0
        self.groups = self.first + self.rest


def list_kernel(plan, group, used, counts, slots, item_tile, item_src, place, over):
    targets, maxs = slots.shape
    per = used // group
    member = lax.rem(lax.axis_index("feat"), group)
    last = plan.slots

    def clear(n, carry):
        item_tile[n] = 0
        item_src[n] = 0
        return carry

    lax.fori_loop(0, last + 1, clear, 0, unroll=8)

    def wipe(n, carry):
        place[n] = -1
        return carry

    lax.fori_loop(0, targets * maxs, wipe, 0, unroll=8)

    following = jnp.int32(0)
    for o in range(group):
        source = lax.rem(member + group - o, group)

        def one_target(t, following, o=o, source=source):
            floor = plan.each * (o * (targets // 2) + t // 2)

            def one_slot(k, following):
                s = slots[t, k]
                mine = (s // per) == source
                slot = jnp.maximum(following, floor)
                at = jnp.minimum(slot, last)
                item_tile[at] = t
                item_src[at] = o * per + lax.rem(s, per)
                n = t * maxs + k
                place[n] = jnp.where(mine, at, place[n])
                return jnp.where(mine, slot + 1, following)

            return lax.fori_loop(0, counts[t], one_slot, following)

        following = lax.fori_loop(0, targets, one_target, following)
    over[0] = (following > last).astype(jnp.int32)


def build_lists(plan, group, used, counts, slots):
    smem = pl.BlockSpec(memory_space=pltpu.SMEM)
    i32 = lambda n: jax.ShapeDtypeStruct((n,), jnp.int32)
    return pl.pallas_call(
        functools.partial(list_kernel, plan, group, used),
        out_shape=[i32(plan.slots + 1), i32(plan.slots + 1), i32(slots.shape[0] * slots.shape[1]), i32(1)],
        in_specs=[smem, smem],
        out_specs=[smem] * 4,
        name="build_lists",
    )(counts, slots)


def edge_kernel(
    plan, group, width,
    item_tile, item_src, over, used_tiles, act, dec, enc, out, any_over,
    raw, table, targets, products, spread, sent, sent_scale, got, got_scale, done, flag, flags,
    raw_sem, load_sem, group_send, group_recv, data_send, data_recv, scale_send, scale_recv, out_sem,
    flag_send, flag_recv,
):
    f, w = lax.axis_index("feat"), lax.axis_index("width")
    feats = flags.shape[0] + 1
    member = lax.rem(f, group)
    layer = f // group
    base = f - member
    members, tile, depth = dec.shape
    per = table.shape[0] // group
    pairs = targets.shape[0] // 2
    rows = tile // width
    parts = depth // PART

    def columns(p):
        return pl.ds(pl.multiple_of(p * PART, PART), PART)

    def raw_load(p, b):
        return pltpu.make_async_copy(dec.at[:, :, columns(p)], raw[b], raw_sem.at[b])

    def pair_load(j):
        two = pl.ds(2 * j, 2)
        return pltpu.make_async_copy(enc.at[two], targets.at[two], load_sem.at[j])

    for b in range(len(raw)):
        raw_load(b, b).start()
    pair_load(0).start()

    barrier = pltpu.get_barrier_semaphore()


    def greet(o, carry):
        pl.semaphore_signal(barrier, 1, device_id=(lax.rem(f + o, feats), w), device_id_type=MESH)
        return carry

    lax.fori_loop(1, feats, greet, 0)
    for o in range(1, width):
        pl.semaphore_signal(barrier, 1, device_id=(f, lax.rem(w + o, width)), device_id_type=MESH)
    pl.semaphore_wait(barrier, feats - 1 + width - 1)

    def group_copy(o, p):
        return pltpu.make_async_remote_copy(
            src_ref=table.at[pl.ds(0, per), :, columns(p)],
            dst_ref=table.at[pl.ds(o * per, per), :, columns(p)],
            send_sem=group_send.at[o - 1, p], recv_sem=group_recv.at[o - 1, p],
            device_id=(base + lax.rem(member + o, group), w), device_id_type=MESH,
        )

    def pick(several, carry):
        for b in range(len(raw)):
            p = several * len(raw) + b
            raw_load(p, b).wait()
            for i in range(per):
                at = lax.rem(used_tiles[layer, member * per + i], members)
                table[i, :, columns(p)] = raw[b][at]
            for o in range(1, group):
                group_copy(o, p).start()

            @pl.when(p + len(raw) < parts)
            def _():
                raw_load(p + len(raw), b).start()

        return carry

    lax.fori_loop(0, parts // len(raw), pick, 0)
    for j in range(1, pairs):
        pair_load(j).start()

    def flag_copy(o):
        return pltpu.make_async_remote_copy(
            src_ref=flag, dst_ref=flags.at[o - 1], send_sem=flag_send.at[o - 1], recv_sem=flag_recv.at[o - 1],
            device_id=(lax.rem(f + o, feats), w), device_id_type=MESH,
        )

    flag[...] = jnp.full(flag.shape, over[0], jnp.int32)

    def tell(o, carry):
        flag_copy(o).start()
        return carry

    lax.fori_loop(1, feats, tell, 0)

    for o in range(group):
        source = lax.rem(member + group - o, group)
        for i in range(per):
            line = act[pl.ds(used_tiles[layer, source * per + i], 1), :]
            spread[o * per + i] = jnp.broadcast_to(line, (tile, tile)).T

    def share(o, g, start, count):
        peer = (f, lax.rem(w + o, width))
        span = pl.ds(start, count)
        data = pltpu.make_async_remote_copy(
            src_ref=sent.at[o - 1, span], dst_ref=got.at[o - 1, span],
            send_sem=data_send.at[o - 1, g], recv_sem=data_recv.at[o - 1, g],
            device_id=peer, device_id_type=MESH,
        )
        scale = pltpu.make_async_remote_copy(
            src_ref=sent_scale.at[o - 1, g], dst_ref=got_scale.at[o - 1, g],
            send_sem=scale_send.at[o - 1, g], recv_sem=scale_recv.at[o - 1, g],
            device_id=peer, device_id_type=MESH,
        )
        return data, scale

    def send(g, start, count):
        for r in range(count):
            n = start + r
            s, t = item_src[n], item_tile[n]
            for o in range(1, width):
                peer = lax.rem(w + o, width)
                part = products[s, t, pl.ds(pl.multiple_of(peer * rows, rows), rows), :]
                peak = jnp.maximum(jnp.max(jnp.abs(part), axis=0, keepdims=True), 1e-30)
                sent[o - 1, n] = jnp.round(part * (TOP / peak)).astype(jnp.int32).astype(jnp.int16)
                sent_scale[o - 1, g, pl.ds(r, 1), :] = peak * (1.0 / TOP)
        for o in range(1, width):
            for copy in share(o, g, start, count):
                copy.start()

    def multiply(o, j):
        left = table[pl.ds(o * per, per)].reshape(per * tile, depth)
        right = targets[pl.ds(2 * j, 2)].reshape(2 * tile, depth)
        value = lax.dot_general(left, right, (((1,), (1,)), ((), ())), preferred_element_type=jnp.float32)
        products[pl.ds(o * per, per), 2 * j] = value[:, :tile].reshape(per, tile, tile)
        products[pl.ds(o * per, per), 2 * j + 1] = value[:, tile:].reshape(per, tile, tile)

    each = plan.each

    def first_step(j, carry):
        pair_load(j).wait()
        multiply(0, j)
        if each:
            send(j, j * each, each)
        return carry

    lax.fori_loop(0, pairs, first_step, 0)

    def phase(o, carry):
        def arrive(p, carry):
            group_copy(o, p).wait_recv()
            return carry

        lax.fori_loop(0, parts, arrive, 0)

        def step(j, carry):
            multiply(o, j)
            if each:
                g = o * pairs + j
                send(g, g * each, each)
            return carry

        lax.fori_loop(0, pairs, step, 0)
        return carry

    lax.fori_loop(1, group, phase, 0)

    def rest_send(g, carry):
        send(plan.first + g, plan.lead + g * CHUNK, CHUNK)
        return carry

    lax.fori_loop(0, plan.rest, rest_send, 0)

    def out_copy(g, start, count):
        span = pl.ds(start, count)
        return pltpu.make_async_copy(done.at[span], out.at[span], out_sem.at[g])

    def finish(g, start, count):
        for o in range(1, width):
            for copy in share(o, g, start, count):
                copy.wait_recv()
        here = pl.ds(pl.multiple_of(w * rows, rows), rows)
        for r in range(count):
            n = start + r
            s, t = item_src[n], item_tile[n]
            total = products[s, t, here, :]
            for o in range(1, width):
                total = total + got[o - 1, n].astype(jnp.int32).astype(jnp.float32) * got_scale[o - 1, g, pl.ds(r, 1), :]
            done[n] = (total * spread[s, here, :]).astype(done.dtype)
        out_copy(g, start, count).start()

    def drain(g, start, count):
        for o in range(1, width):
            for copy in share(o, g, start, count):
                copy.wait_send()
        out_copy(g, start, count).wait()

    def over_groups(act_on):
        def lead(g, carry):
            act_on(g, g * each, each)
            return carry

        def rest(g, carry):
            act_on(plan.first + g, plan.lead + g * CHUNK, CHUNK)
            return carry

        if plan.first:
            lax.fori_loop(0, plan.first, lead, 0)
        lax.fori_loop(0, plan.rest, rest, 0)

    over_groups(finish)
    over_groups(drain)

    def hear(o, highest):
        flag_copy(o).wait()
        return jnp.maximum(highest, flags[o - 1])

    any_over[0] = jnp.max(lax.fori_loop(1, feats, hear, flag[...]))

    def group_drain(p, carry):
        for o in range(1, group):
            group_copy(o, p).wait_send()
        return carry

    lax.fori_loop(0, parts, group_drain, 0)


def edges_of(plan, number, group, width, item_tile, item_src, over, used_tiles, act, dec, enc):
    members, tile, depth = dec.shape
    used = used_tiles.shape[1]
    targets = enc.shape[0]
    rows = tile // width
    others = width - 1
    parts = depth // PART
    feats = lax.axis_size("feat")
    flag_kind = (8, 128)
    smem = pl.BlockSpec(memory_space=pltpu.SMEM)
    vmem = pl.BlockSpec(memory_space=pltpu.VMEM)
    hbm = pl.BlockSpec(memory_space=pl.ANY)
    return pl.pallas_call(
        functools.partial(edge_kernel, plan, group, width),
        out_shape=[
            jax.ShapeDtypeStruct((plan.slots, rows, tile), jnp.bfloat16),
            jax.ShapeDtypeStruct((1,), jnp.int32),
        ],
        in_specs=[smem, smem, smem, smem, vmem, hbm, hbm],
        out_specs=[hbm, smem],
        scratch_shapes=[
            [pltpu.VMEM((members, tile, PART), jnp.bfloat16)] * min(RAW, parts),
            pltpu.VMEM((used, tile, depth), jnp.bfloat16),
            pltpu.VMEM((targets, tile, depth), jnp.bfloat16),
            pltpu.VMEM((used, targets, tile, tile), jnp.float32),
            pltpu.VMEM((used, tile, tile), jnp.float32),
            pltpu.VMEM((others, plan.slots, rows, tile), jnp.int16),
            pltpu.VMEM((others, plan.groups, CHUNK, tile), jnp.float32),
            pltpu.VMEM((others, plan.slots, rows, tile), jnp.int16),
            pltpu.VMEM((others, plan.groups, CHUNK, tile), jnp.float32),
            pltpu.VMEM((plan.slots, rows, tile), jnp.bfloat16),
            pltpu.VMEM(flag_kind, jnp.int32),
            pltpu.VMEM((feats - 1,) + flag_kind, jnp.int32),
            DMA((RAW,)),
            DMA((targets // 2,)),
            DMA((max(group - 1, 1), parts)),
            DMA((max(group - 1, 1), parts)),
            DMA((others, plan.groups)),
            DMA((others, plan.groups)),
            DMA((others, plan.groups)),
            DMA((others, plan.groups)),
            DMA((plan.groups,)),
            DMA((feats - 1,)),
            DMA((feats - 1,)),
        ],
        compiler_params=pltpu.CompilerParams(
            collective_id=number, has_side_effects=True, vmem_limit_bytes=63 * 2**20
        ),
        name=f"edges_{plan.slots}",
    )(item_tile, item_src, over, used_tiles, act, dec, enc)


def place_kernel(place, packed, out, held, full, in_sem, out_sem):
    targets, slots = full.shape[:2]
    load = pltpu.make_async_copy(packed, held, in_sem)
    load.start()
    load.wait()

    def leave(t):
        return pltpu.make_async_copy(full.at[t], out.at[t], out_sem.at[t])

    def one(t, carry):
        for k in range(slots):
            at = place[t * slots + k]
            value = held[jnp.maximum(at, 0)]
            full[t, k] = jnp.where(at >= 0, value, jnp.zeros_like(value))
        leave(t).start()
        return carry

    lax.fori_loop(0, targets, one, 0)

    def drain(t, carry):
        leave(t).wait()
        return carry

    lax.fori_loop(0, targets, drain, 0)


def place_tiles(targets, slots, place, packed):
    rows, tile = packed.shape[1:]
    shape = (targets, slots, rows, tile)
    hbm = pl.BlockSpec(memory_space=pl.ANY)
    return pl.pallas_call(
        place_kernel,
        out_shape=jax.ShapeDtypeStruct(shape, packed.dtype),
        in_specs=[pl.BlockSpec(memory_space=pltpu.SMEM), hbm],
        out_specs=hbm,
        scratch_shapes=[
            pltpu.VMEM(packed.shape, packed.dtype),
            pltpu.VMEM(shape, packed.dtype),
            DMA,
            DMA((targets,)),
        ],
        compiler_params=pltpu.CompilerParams(vmem_limit_bytes=32 * 2**20),
        name="place_tiles",
    )(place, packed)


def on_device(dec_rows, enc_rows, src_act, src_slots, counts, used_tiles):
    layers, used = used_tiles.shape
    group = lax.axis_size("feat") // layers
    width = lax.axis_size("width")
    targets, maxs = src_slots.shape
    tile = enc_rows.shape[0] // targets
    depth = dec_rows.shape[1]
    members = dec_rows.shape[0] // tile
    dec = dec_rows.reshape(members, tile, depth)
    enc = enc_rows.reshape(targets, tile, depth)
    act = src_act.reshape(-1, tile)
    steps = group * (targets // 2)
    slots = targets * maxs

    usual = Plan(steps, slots * 17 // 24, 0.84)
    item_tile, item_src, place, over = build_lists(usual, group, used, counts, src_slots)
    packed, any_over = edges_of(usual, 0, group, width, item_tile, item_src, over, used_tiles, act, dec, enc)

    def fits(packed, place):
        return place_tiles(targets, maxs, place, packed)

    def exceeds(packed, place):
        whole = Plan(steps, slots, 0.0)
        item_tile, item_src, place, over = build_lists(whole, group, used, counts, src_slots)
        packed, _ = edges_of(whole, 1, group, width, item_tile, item_src, over, used_tiles, act, dec, enc)
        return place_tiles(targets, maxs, place, packed)

    return lax.cond(any_over[0] > 0, exceeds, fits, packed, place)


def solution(mesh):
    return jax.shard_map(
        on_device,
        mesh=mesh,
        in_specs=(P("feat", "width"), P("feat", "width"), P(), P("feat", None), P("feat"), P()),
        out_specs=P("feat", None, "width", None),
        check_vma=False,
    )
```

```python
import functools

import jax
import jax.numpy as jnp
from jax import lax
from jax.experimental import pallas as pl
from jax.experimental.pallas import tpu as pltpu
from jax.sharding import PartitionSpec as P

CHUNK = 8
TOP = 32767.0
MESH = pl.DeviceIdType.MESH
DMA = pltpu.SemaphoreType.DMA
PART = 256
RAW = 4


class Plan:
    def __init__(self, steps, wanted, share):
        self.steps = steps
        self.each = min(int(wanted * share) // steps, CHUNK)
        self.rest = -(-(wanted - self.each * steps) // CHUNK)
        self.lead = self.each * steps
        self.slots = self.lead + self.rest * CHUNK
        self.first = steps if self.each else 0
        self.groups = self.first + self.rest


def edge_kernel(
    plan, group, width,
    counts, slots, used_tiles, act, dec, enc, out, place, any_over,
    raw, table, targets, products, spread, sent, sent_scale, got, got_scale, done, flag, flags, item_rows, items,
    item_sem, raw_sem, load_sem, group_send, group_recv, data_send, data_recv, scale_send, scale_recv, out_sem,
    flag_send, flag_recv,
):
    f, w = lax.axis_index("feat"), lax.axis_index("width")
    feats = flags.shape[0] + 1
    member = lax.rem(f, group)
    layer = f // group
    base = f - member
    members, tile, depth = dec.shape
    per = table.shape[0] // group
    pairs = targets.shape[0] // 2
    rows = tile // width
    parts = depth // PART

    def columns(p):
        return pl.ds(pl.multiple_of(p * PART, PART), PART)

    def raw_load(p, b):
        return pltpu.make_async_copy(dec.at[:, :, columns(p)], raw[b], raw_sem.at[b])

    def pair_load(j):
        two = pl.ds(2 * j, 2)
        return pltpu.make_async_copy(enc.at[two], targets.at[two], load_sem.at[j])

    pair_load(0).start()
    for b in range(len(raw)):
        raw_load(b, b).start()

    barrier = pltpu.get_barrier_semaphore()


    def greet(o, carry):
        pl.semaphore_signal(barrier, 1, device_id=(lax.rem(f + o, feats), w), device_id_type=MESH)
        return carry

    lax.fori_loop(1, feats, greet, 0)
    for o in range(1, width):
        pl.semaphore_signal(barrier, 1, device_id=(f, lax.rem(w + o, width)), device_id_type=MESH)

    number = lax.broadcasted_iota(jnp.int32, item_rows.shape, 0) * item_rows.shape[1]
    number = number + lax.broadcasted_iota(jnp.int32, item_rows.shape, 1)
    tiles, maxs = slots.shape
    listed, following = jnp.zeros(item_rows.shape, jnp.int32), jnp.int32(0)
    for o in range(group):
        source = lax.rem(member + group - o, group)

        def one_target(t, carry, o=o, source=source):
            listed, following = carry
            floor = plan.each * (o * pairs + t // 2)
            live = counts[t]
            for k in range(maxs):
                s = slots[t, k]
                mine = jnp.logical_and(s // per == source, k < live)
                slot = jnp.maximum(following, floor)
                code = (o * per + lax.rem(s, per)) * tiles + t
                listed = jnp.where(number == jnp.where(mine, slot, -1), code, listed)
                n = t * maxs + k
                place[n] = jnp.where(mine, slot, -1 if o == 0 else place[n])
                following = jnp.where(mine, slot + 1, following)
            return listed, following

        listed, following = lax.fori_loop(0, tiles, one_target, (listed, following))
    item_rows[...] = listed
    to_items = pltpu.make_async_copy(item_rows, items, item_sem)
    to_items.start()
    over = (following > plan.slots).astype(jnp.int32)

    def item(n):
        code = items[n // items.shape[1], lax.rem(n, items.shape[1])]
        return code // tiles, lax.rem(code, tiles)

    products[pl.ds(0, per), pl.ds(0, 2)] = jnp.zeros((per, 2, tile, tile), jnp.float32)
    pl.semaphore_wait(barrier, feats - 1 + width - 1)

    def group_copy(o, p):
        return pltpu.make_async_remote_copy(
            src_ref=table.at[pl.ds(0, per), :, columns(p)],
            dst_ref=table.at[pl.ds(o * per, per), :, columns(p)],
            send_sem=group_send.at[o - 1, p], recv_sem=group_recv.at[o - 1, p],
            device_id=(base + lax.rem(member + o, group), w), device_id_type=MESH,
        )

    pair_load(0).wait()

    def pick(several, carry):
        for b in range(len(raw)):
            p = several * len(raw) + b
            raw_load(p, b).wait()
            for i in range(per):
                at = lax.rem(used_tiles[layer, member * per + i], members)
                table[i, :, columns(p)] = raw[b][at]
            for o in range(1, group):
                group_copy(o, p).start()

            @pl.when(p + len(raw) < parts)
            def _():
                raw_load(p + len(raw), b).start()

            if b % 2:
                both = pl.ds(pl.multiple_of((p - 1) * PART, PART), 2 * PART)
                left = table[pl.ds(0, per), :, both].reshape(per * tile, 2 * PART)
                right = targets[pl.ds(0, 2), :, both].reshape(2 * tile, 2 * PART)
                value = lax.dot_general(left, right, (((1,), (1,)), ((), ())), preferred_element_type=jnp.float32)
                products[pl.ds(0, per), 0] += value[:, :tile].reshape(per, tile, tile)
                products[pl.ds(0, per), 1] += value[:, tile:].reshape(per, tile, tile)

        if pairs > 1:
            @pl.when(several == parts // len(raw) // 2)
            def _():
                pair_load(1).start()

        return carry

    lax.fori_loop(0, parts // len(raw), pick, 0)
    for j in range(2, pairs):
        pair_load(j).start()

    def share(o, g, start, count):
        peer = (f, lax.rem(w + o, width))
        span = pl.ds(start, count)
        data = pltpu.make_async_remote_copy(
            src_ref=sent.at[o - 1, span], dst_ref=got.at[o - 1, span],
            send_sem=data_send.at[o - 1, g], recv_sem=data_recv.at[o - 1, g],
            device_id=peer, device_id_type=MESH,
        )
        scale = pltpu.make_async_remote_copy(
            src_ref=sent_scale.at[o - 1, g], dst_ref=got_scale.at[o - 1, g],
            send_sem=scale_send.at[o - 1, g], recv_sem=scale_recv.at[o - 1, g],
            device_id=peer, device_id_type=MESH,
        )
        return data, scale

    def send(g, start, count):
        for r in range(count):
            n = start + r
            s, t = item(n)
            for o in range(1, width):
                peer = lax.rem(w + o, width)
                part = products[s, t, pl.ds(pl.multiple_of(peer * rows, rows), rows), :]
                peak = jnp.maximum(jnp.max(jnp.abs(part), axis=0, keepdims=True), 1e-30)
                sent[o - 1, n] = jnp.round(part * (TOP / peak)).astype(jnp.int32).astype(jnp.int16)
                sent_scale[o - 1, g, pl.ds(r, 1), :] = peak * (1.0 / TOP)
        for o in range(1, width):
            for copy in share(o, g, start, count):
                copy.start()

    def multiply(o, j):
        left = table[pl.ds(o * per, per)].reshape(per * tile, depth)
        right = targets[pl.ds(2 * j, 2)].reshape(2 * tile, depth)
        value = lax.dot_general(left, right, (((1,), (1,)), ((), ())), preferred_element_type=jnp.float32)
        products[pl.ds(o * per, per), 2 * j] = value[:, :tile].reshape(per, tile, tile)
        products[pl.ds(o * per, per), 2 * j + 1] = value[:, tile:].reshape(per, tile, tile)

    each = plan.each

    def first_step(j, carry):
        pair_load(j).wait()
        multiply(0, j)
        if each:
            send(j, j * each, each)
        return carry

    to_items.wait()
    if each:
        send(0, 0, each)
    lax.fori_loop(1, pairs, first_step, 0)

    def phase(o, carry):
        def arrive(p, carry):
            group_copy(o, p).wait_recv()
            return carry

        lax.fori_loop(0, parts, arrive, 0)

        def step(j, carry):
            multiply(o, j)
            if each:
                g = o * pairs + j
                send(g, g * each, each)
            return carry

        lax.fori_loop(0, pairs, step, 0)
        return carry

    lax.fori_loop(1, group, phase, 0)

    def rest_send(g, carry):
        send(plan.first + g, plan.lead + g * CHUNK, CHUNK)
        return carry

    lax.fori_loop(0, plan.rest, rest_send, 0)

    def flag_copy(o):
        return pltpu.make_async_remote_copy(
            src_ref=flag, dst_ref=flags.at[o - 1], send_sem=flag_send.at[o - 1], recv_sem=flag_recv.at[o - 1],
            device_id=(lax.rem(f + o, feats), w), device_id_type=MESH,
        )

    flag[...] = jnp.full(flag.shape, over, jnp.int32)

    def tell(o, carry):
        flag_copy(o).start()
        return carry

    lax.fori_loop(1, feats, tell, 0)

    for o in range(group):
        source = lax.rem(member + group - o, group)
        for i in range(per):
            line = act[pl.ds(used_tiles[layer, source * per + i], 1), :]
            spread[o * per + i] = jnp.broadcast_to(line, (tile, tile)).T

    def out_copy(g, start, count):
        span = pl.ds(start, count)
        return pltpu.make_async_copy(done.at[span], out.at[span], out_sem.at[g])

    def finish(g, start, count):
        for o in range(1, width):
            for copy in share(o, g, start, count):
                copy.wait_recv()
        here = pl.ds(pl.multiple_of(w * rows, rows), rows)
        for r in range(count):
            n = start + r
            s, t = item(n)
            total = products[s, t, here, :]
            for o in range(1, width):
                total = total + got[o - 1, n].astype(jnp.int32).astype(jnp.float32) * got_scale[o - 1, g, pl.ds(r, 1), :]
            done[n] = (total * spread[s, here, :]).astype(done.dtype)
        out_copy(g, start, count).start()

    def drain(g, start, count):
        for o in range(1, width):
            for copy in share(o, g, start, count):
                copy.wait_send()
        out_copy(g, start, count).wait()

    def over_groups(act_on):
        def lead(g, carry):
            act_on(g, g * each, each)
            return carry

        def rest(g, carry):
            act_on(plan.first + g, plan.lead + g * CHUNK, CHUNK)
            return carry

        if plan.first:
            lax.fori_loop(0, plan.first, lead, 0)
        lax.fori_loop(0, plan.rest, rest, 0)

    over_groups(finish)
    over_groups(drain)

    def hear(o, highest):
        flag_copy(o).wait()
        return jnp.maximum(highest, flags[o - 1])

    any_over[0] = jnp.max(lax.fori_loop(1, feats, hear, flag[...]))

    def group_drain(p, carry):
        for o in range(1, group):
            group_copy(o, p).wait_send()
        return carry

    lax.fori_loop(0, parts, group_drain, 0)


def edges_of(plan, number, group, width, counts, slots, used_tiles, act, dec, enc):
    members, tile, depth = dec.shape
    used = used_tiles.shape[1]
    targets = enc.shape[0]
    rows = tile // width
    others = width - 1
    parts = depth // PART
    feats = lax.axis_size("feat")
    flag_kind = (8, 128)
    smem = pl.BlockSpec(memory_space=pltpu.SMEM)
    vmem = pl.BlockSpec(memory_space=pltpu.VMEM)
    hbm = pl.BlockSpec(memory_space=pl.ANY)
    return pl.pallas_call(
        functools.partial(edge_kernel, plan, group, width),
        out_shape=[
            jax.ShapeDtypeStruct((plan.slots, rows, tile), jnp.bfloat16),
            jax.ShapeDtypeStruct((slots.shape[0] * slots.shape[1],), jnp.int32),
            jax.ShapeDtypeStruct((1,), jnp.int32),
        ],
        in_specs=[smem, smem, smem, vmem, hbm, hbm],
        out_specs=[hbm, smem, smem],
        scratch_shapes=[
            [pltpu.VMEM((members, tile, PART), jnp.bfloat16)] * min(RAW, parts),
            pltpu.VMEM((used, tile, depth), jnp.bfloat16),
            pltpu.VMEM((targets, tile, depth), jnp.bfloat16),
            pltpu.VMEM((used, targets, tile, tile), jnp.float32),
            pltpu.VMEM((used, tile, tile), jnp.float32),
            pltpu.VMEM((others, plan.slots, rows, tile), jnp.int16),
            pltpu.VMEM((others, plan.groups, CHUNK, tile), jnp.float32),
            pltpu.VMEM((others, plan.slots, rows, tile), jnp.int16),
            pltpu.VMEM((others, plan.groups, CHUNK, tile), jnp.float32),
            pltpu.VMEM((plan.slots, rows, tile), jnp.bfloat16),
            pltpu.VMEM(flag_kind, jnp.int32),
            pltpu.VMEM((feats - 1,) + flag_kind, jnp.int32),
            pltpu.VMEM(flag_kind, jnp.int32),
            pltpu.SMEM(flag_kind, jnp.int32),
            DMA,
            DMA((RAW,)),
            DMA((targets // 2,)),
            DMA((max(group - 1, 1), parts)),
            DMA((max(group - 1, 1), parts)),
            DMA((others, plan.groups)),
            DMA((others, plan.groups)),
            DMA((others, plan.groups)),
            DMA((others, plan.groups)),
            DMA((plan.groups,)),
            DMA((feats - 1,)),
            DMA((feats - 1,)),
        ],
        compiler_params=pltpu.CompilerParams(
            collective_id=number, has_side_effects=True, vmem_limit_bytes=63 * 2**20
        ),
        name=f"edges_{plan.slots}",
    )(counts, slots, used_tiles, act, dec, enc)


def place_kernel(place, packed, out, held, full, in_sem, out_sem):
    targets, slots = full.shape[:2]
    load = pltpu.make_async_copy(packed, held, in_sem)
    load.start()
    load.wait()

    def leave(t):
        return pltpu.make_async_copy(full.at[t], out.at[t], out_sem.at[t])

    def one(t, carry):
        for k in range(slots):
            at = place[t * slots + k]
            value = held[jnp.maximum(at, 0)]
            full[t, k] = jnp.where(at >= 0, value, jnp.zeros_like(value))
        leave(t).start()
        return carry

    lax.fori_loop(0, targets, one, 0)

    def drain(t, carry):
        leave(t).wait()
        return carry

    lax.fori_loop(0, targets, drain, 0)


def place_tiles(targets, slots, place, packed):
    rows, tile = packed.shape[1:]
    shape = (targets, slots, rows, tile)
    hbm = pl.BlockSpec(memory_space=pl.ANY)
    return pl.pallas_call(
        place_kernel,
        out_shape=jax.ShapeDtypeStruct(shape, packed.dtype),
        in_specs=[pl.BlockSpec(memory_space=pltpu.SMEM), hbm],
        out_specs=hbm,
        scratch_shapes=[
            pltpu.VMEM(packed.shape, packed.dtype),
            pltpu.VMEM(shape, packed.dtype),
            DMA,
            DMA((targets,)),
        ],
        compiler_params=pltpu.CompilerParams(vmem_limit_bytes=32 * 2**20),
        name="place_tiles",
    )(place, packed)


def on_device(dec_rows, enc_rows, src_act, src_slots, counts, used_tiles):
    layers, used = used_tiles.shape
    group = lax.axis_size("feat") // layers
    width = lax.axis_size("width")
    targets, maxs = src_slots.shape
    tile = enc_rows.shape[0] // targets
    depth = dec_rows.shape[1]
    members = dec_rows.shape[0] // tile
    dec = dec_rows.reshape(members, tile, depth)
    enc = enc_rows.reshape(targets, tile, depth)
    act = src_act.reshape(-1, tile)
    steps = group * (targets // 2)
    slots = targets * maxs

    usual = Plan(steps, slots * 17 // 24, 0.84)
    def run(plan, number):
        return edges_of(plan, number, group, width, counts, src_slots, used_tiles, act, dec, enc)

    packed, place, any_over = run(usual, 0)

    def fits(packed, place):
        return place_tiles(targets, maxs, place, packed)

    def exceeds(packed, place):
        packed, place, _ = run(Plan(steps, slots, 0.0), 1)
        return place_tiles(targets, maxs, place, packed)

    return lax.cond(any_over[0] > 0, exceeds, fits, packed, place)


def solution(mesh):
    return jax.shard_map(
        on_device,
        mesh=mesh,
        in_specs=(P("feat", "width"), P("feat", "width"), P(), P("feat", None), P("feat"), P()),
        out_specs=P("feat", None, "width", None),
        check_vma=False,
    )
```

```python
import functools

import jax
import jax.numpy as jnp
from jax import lax
from jax.experimental import pallas as pl
from jax.experimental.pallas import tpu as pltpu
from jax.sharding import PartitionSpec as P

CHUNK = 8
TOP = 32767.0
MESH = pl.DeviceIdType.MESH
DMA = pltpu.SemaphoreType.DMA
PART = 256
RAW = 4


class Plan:
    def __init__(self, steps, wanted, share):
        self.steps = steps
        self.each = min(int(wanted * share) // steps, CHUNK)
        self.rest = -(-(wanted - self.each * steps) // CHUNK)
        self.lead = self.each * steps
        self.slots = self.lead + self.rest * CHUNK
        self.first = steps if self.each else 0
        self.groups = self.first + self.rest


def edge_kernel(
    plan, group, width,
    counts_in, slots_in, used_in, act_in, dec, enc, out, place_out, any_over_out,
    counts, slots, used_tiles, act, place, any_over,
    raw, table, targets, products, spread, sent, sent_scale, got, got_scale, done, flag, flags, item_rows, items,
    small_sem, item_sem, raw_sem, load_sem, group_send, group_recv, data_send, data_recv, scale_send, scale_recv, out_sem,
    flag_send, flag_recv,
):
    f, w = lax.axis_index("feat"), lax.axis_index("width")
    feats = flags.shape[0] + 1
    member = lax.rem(f, group)
    layer = f // group
    base = f - member
    members, tile, depth = dec.shape
    per = table.shape[0] // group
    pairs = targets.shape[0] // 2
    rows = tile // width
    parts = depth // PART

    def columns(p):
        return pl.ds(pl.multiple_of(p * PART, PART), PART)

    def raw_load(p, b):
        return pltpu.make_async_copy(dec.at[:, :, columns(p)], raw[b], raw_sem.at[b])

    def pair_load(j):
        two = pl.ds(2 * j, 2)
        return pltpu.make_async_copy(enc.at[two], targets.at[two], load_sem.at[j])

    for b in range(len(raw)):
        raw_load(b, b).start()
    small = [
        pltpu.make_async_copy(source, held, small_sem.at[i])
        for i, (source, held) in enumerate(
            ((used_in, used_tiles), (counts_in, counts), (slots_in, slots), (act_in, act))
        )
    ]
    for load in small:
        load.start()
    pair_load(0).start()

    barrier = pltpu.get_barrier_semaphore()


    def greet(o, carry):
        pl.semaphore_signal(barrier, 1, device_id=(lax.rem(f + o, feats), w), device_id_type=MESH)
        return carry

    lax.fori_loop(1, feats, greet, 0)
    for o in range(1, width):
        pl.semaphore_signal(barrier, 1, device_id=(f, lax.rem(w + o, width)), device_id_type=MESH)

    number = lax.broadcasted_iota(jnp.int32, item_rows.shape, 0) * item_rows.shape[1]
    number = number + lax.broadcasted_iota(jnp.int32, item_rows.shape, 1)
    tiles, maxs = slots.shape

    def list_target(at, carry):
        listed, following = carry
        o, t = at // tiles, lax.rem(at, tiles)
        source = lax.rem(member + group - o, group)
        floor = plan.each * (o * pairs + t // 2)
        live = counts[t]
        for k in range(maxs):
            s = slots[t, k]
            mine = jnp.logical_and(s // per == source, k < live)
            slot = jnp.maximum(following, floor)
            code = (o * per + lax.rem(s, per)) * tiles + t
            listed = jnp.where(number == jnp.where(mine, slot, -1), code, listed)
            n = t * maxs + k
            place[n] = jnp.where(mine, slot, jnp.where(o == 0, -1, place[n]))
            following = jnp.where(mine, slot + 1, following)
        return listed, following

    to_items = pltpu.make_async_copy(item_rows, items, item_sem)

    def item(n):
        code = items[n // items.shape[1], lax.rem(n, items.shape[1])]
        return code // tiles, lax.rem(code, tiles)

    products[pl.ds(0, per), pl.ds(0, 2)] = jnp.zeros((per, 2, tile, tile), jnp.float32)
    pl.semaphore_wait(barrier, feats - 1 + width - 1)

    def group_copy(o, p):
        return pltpu.make_async_remote_copy(
            src_ref=table.at[pl.ds(0, per), :, columns(p)],
            dst_ref=table.at[pl.ds(o * per, per), :, columns(p)],
            send_sem=group_send.at[o - 1, p], recv_sem=group_recv.at[o - 1, p],
            device_id=(base + lax.rem(member + o, group), w), device_id_type=MESH,
        )

    for load in small:
        load.wait()

    def pick(several, carry):
        for b in range(len(raw)):
            p = several * len(raw) + b
            raw_load(p, b).wait()
            for i in range(per):
                at = lax.rem(used_tiles[layer, member * per + i], members)
                table[i, :, columns(p)] = raw[b][at]
            for o in range(1, group):
                group_copy(o, p).start()

            @pl.when(p + len(raw) < parts)
            def _():
                raw_load(p + len(raw), b).start()

        @pl.when(several == 0)
        def _():
            pair_load(0).wait()

        run = len(raw) * PART
        these = pl.ds(pl.multiple_of(several * run, run), run)
        left = table[pl.ds(0, per), :, these].reshape(per * tile, run)
        right = targets[pl.ds(0, 2), :, these].reshape(2 * tile, run)
        value = lax.dot_general(left, right, (((1,), (1,)), ((), ())), preferred_element_type=jnp.float32)
        products[pl.ds(0, per), 0] += value[:, :tile].reshape(per, tile, tile)
        products[pl.ds(0, per), 1] += value[:, tile:].reshape(per, tile, tile)
        carry = lax.fori_loop(several * portion, (several + 1) * portion, list_target, carry)

        if pairs > 1:
            @pl.when(several == parts // len(raw) // 2)
            def _():
                pair_load(1).start()

        return carry

    rounds = parts // len(raw)
    portion = group * tiles // rounds
    start = (jnp.zeros(item_rows.shape, jnp.int32), jnp.int32(0))
    listed, following = lax.fori_loop(0, rounds, pick, start)
    listed, following = lax.fori_loop(rounds * portion, group * tiles, list_target, (listed, following))
    over = (following > plan.slots).astype(jnp.int32)
    item_rows[...] = listed
    to_items.start()
    give_place = pltpu.make_async_copy(place, place_out, small_sem.at[0])
    give_place.start()
    for j in range(2, pairs):
        pair_load(j).start()

    def share(o, g, start, count):
        peer = (f, lax.rem(w + o, width))
        span = pl.ds(start, count)
        data = pltpu.make_async_remote_copy(
            src_ref=sent.at[o - 1, span], dst_ref=got.at[o - 1, span],
            send_sem=data_send.at[o - 1, g], recv_sem=data_recv.at[o - 1, g],
            device_id=peer, device_id_type=MESH,
        )
        scale = pltpu.make_async_remote_copy(
            src_ref=sent_scale.at[o - 1, g], dst_ref=got_scale.at[o - 1, g],
            send_sem=scale_send.at[o - 1, g], recv_sem=scale_recv.at[o - 1, g],
            device_id=peer, device_id_type=MESH,
        )
        return data, scale

    def send(g, start, count):
        for r in range(count):
            n = start + r
            s, t = item(n)
            for o in range(1, width):
                peer = lax.rem(w + o, width)
                part = products[s, t, pl.ds(pl.multiple_of(peer * rows, rows), rows), :]
                peak = jnp.maximum(jnp.max(jnp.abs(part), axis=0, keepdims=True), 1e-30)
                sent[o - 1, n] = jnp.round(part * (TOP / peak)).astype(jnp.int32).astype(jnp.int16)
                sent_scale[o - 1, g, pl.ds(r, 1), :] = peak * (1.0 / TOP)
        for o in range(1, width):
            for copy in share(o, g, start, count):
                copy.start()

    def multiply(o, j):
        left = table[pl.ds(o * per, per)].reshape(per * tile, depth)
        right = targets[pl.ds(2 * j, 2)].reshape(2 * tile, depth)
        value = lax.dot_general(left, right, (((1,), (1,)), ((), ())), preferred_element_type=jnp.float32)
        products[pl.ds(o * per, per), 2 * j] = value[:, :tile].reshape(per, tile, tile)
        products[pl.ds(o * per, per), 2 * j + 1] = value[:, tile:].reshape(per, tile, tile)

    each = plan.each

    def first_step(j, carry):
        pair_load(j).wait()
        multiply(0, j)
        if each:
            send(j, j * each, each)
        return carry

    to_items.wait()
    if each:
        send(0, 0, each)
    lax.fori_loop(1, pairs, first_step, 0)

    def phase(o, carry):
        def arrive(p, carry):
            group_copy(o, p).wait_recv()
            return carry

        lax.fori_loop(0, parts, arrive, 0)

        def step(j, carry):
            multiply(o, j)
            if each:
                g = o * pairs + j
                send(g, g * each, each)
            return carry

        lax.fori_loop(0, pairs, step, 0)
        return carry

    lax.fori_loop(1, group, phase, 0)

    def rest_send(g, carry):
        send(plan.first + g, plan.lead + g * CHUNK, CHUNK)
        return carry

    lax.fori_loop(0, plan.rest, rest_send, 0)

    def flag_copy(o):
        return pltpu.make_async_remote_copy(
            src_ref=flag, dst_ref=flags.at[o - 1], send_sem=flag_send.at[o - 1], recv_sem=flag_recv.at[o - 1],
            device_id=(lax.rem(f + o, feats), w), device_id_type=MESH,
        )

    flag[...] = jnp.full(flag.shape, over, jnp.int32)

    def tell(o, carry):
        flag_copy(o).start()
        return carry

    lax.fori_loop(1, feats, tell, 0)

    for o in range(group):
        source = lax.rem(member + group - o, group)
        for i in range(per):
            line = act[pl.ds(used_tiles[layer, source * per + i], 1), :]
            spread[o * per + i] = jnp.broadcast_to(line, (tile, tile)).T

    def out_copy(g, start, count):
        span = pl.ds(start, count)
        return pltpu.make_async_copy(done.at[span], out.at[span], out_sem.at[g])

    def finish(g, start, count):
        for o in range(1, width):
            for copy in share(o, g, start, count):
                copy.wait_recv()
        here = pl.ds(pl.multiple_of(w * rows, rows), rows)
        for r in range(count):
            n = start + r
            s, t = item(n)
            total = products[s, t, here, :]
            for o in range(1, width):
                total = total + got[o - 1, n].astype(jnp.int32).astype(jnp.float32) * got_scale[o - 1, g, pl.ds(r, 1), :]
            done[n] = (total * spread[s, here, :]).astype(done.dtype)
        out_copy(g, start, count).start()

    def drain(g, start, count):
        for o in range(1, width):
            for copy in share(o, g, start, count):
                copy.wait_send()
        out_copy(g, start, count).wait()

    def lead(act_on):
        def one(g, carry):
            act_on(g, g * each, each)
            return carry

        lax.fori_loop(0, plan.first, one, 0)

    def rest(act_on, first, last):
        def one(g, carry):
            act_on(plan.first + g, plan.lead + g * CHUNK, CHUNK)
            return carry

        lax.fori_loop(first, last, one, 0)

    if plan.first:
        lead(finish)
    rest(finish, 0, plan.rest - 1)
    if plan.first:
        lead(drain)
    rest(drain, 0, plan.rest - 1)

    def group_drain(p, carry):
        for o in range(1, group):
            group_copy(o, p).wait_send()
        return carry

    lax.fori_loop(0, parts, group_drain, 0)

    def hear(o, highest):
        flag_copy(o).wait()
        return jnp.maximum(highest, flags[o - 1])

    any_over[0] = jnp.max(lax.fori_loop(1, feats, hear, flag[...]))
    give_over = pltpu.make_async_copy(any_over, any_over_out, small_sem.at[1])
    give_over.start()
    rest(finish, plan.rest - 1, plan.rest)
    give_place.wait()
    give_over.wait()
    rest(drain, plan.rest - 1, plan.rest)


def edges_of(plan, number, group, width, counts, slots, used_tiles, act, dec, enc):
    members, tile, depth = dec.shape
    used = used_tiles.shape[1]
    targets = enc.shape[0]
    rows = tile // width
    others = width - 1
    parts = depth // PART
    feats = lax.axis_size("feat")
    flag_kind = (8, 128)
    hbm = pl.BlockSpec(memory_space=pl.ANY)
    return pl.pallas_call(
        functools.partial(edge_kernel, plan, group, width),
        out_shape=[
            jax.ShapeDtypeStruct((plan.slots, rows, tile), jnp.bfloat16),
            jax.ShapeDtypeStruct((slots.shape[0] * slots.shape[1],), jnp.int32),
            jax.ShapeDtypeStruct((1,), jnp.int32),
        ],
        in_specs=[hbm] * 6,
        out_specs=[hbm] * 3,
        scratch_shapes=[
            pltpu.SMEM(counts.shape, jnp.int32),
            pltpu.SMEM(slots.shape, jnp.int32),
            pltpu.SMEM(used_tiles.shape, jnp.int32),
            pltpu.VMEM(act.shape, jnp.float32),
            pltpu.SMEM((slots.shape[0] * slots.shape[1],), jnp.int32),
            pltpu.SMEM((1,), jnp.int32),
            [pltpu.VMEM((members, tile, PART), jnp.bfloat16)] * min(RAW, parts),
            pltpu.VMEM((used, tile, depth), jnp.bfloat16),
            pltpu.VMEM((targets, tile, depth), jnp.bfloat16),
            pltpu.VMEM((used, targets, tile, tile), jnp.float32),
            pltpu.VMEM((used, tile, tile), jnp.float32),
            pltpu.VMEM((others, plan.slots, rows, tile), jnp.int16),
            pltpu.VMEM((others, plan.groups, CHUNK, tile), jnp.float32),
            pltpu.VMEM((others, plan.slots, rows, tile), jnp.int16),
            pltpu.VMEM((others, plan.groups, CHUNK, tile), jnp.float32),
            pltpu.VMEM((plan.slots, rows, tile), jnp.bfloat16),
            pltpu.VMEM(flag_kind, jnp.int32),
            pltpu.VMEM((feats - 1,) + flag_kind, jnp.int32),
            pltpu.VMEM(flag_kind, jnp.int32),
            pltpu.SMEM(flag_kind, jnp.int32),
            DMA((4,)),
            DMA,
            DMA((RAW,)),
            DMA((targets // 2,)),
            DMA((max(group - 1, 1), parts)),
            DMA((max(group - 1, 1), parts)),
            DMA((others, plan.groups)),
            DMA((others, plan.groups)),
            DMA((others, plan.groups)),
            DMA((others, plan.groups)),
            DMA((plan.groups,)),
            DMA((feats - 1,)),
            DMA((feats - 1,)),
        ],
        compiler_params=pltpu.CompilerParams(
            collective_id=number, has_side_effects=True, vmem_limit_bytes=(63 if number else 60) * 2**20
        ),
        name=f"edges_{plan.slots}",
    )(counts, slots, used_tiles, act, dec, enc)


def place_kernel(place, packed, out, full, out_sem):
    targets, slots = full.shape[:2]

    def leave(t):
        return pltpu.make_async_copy(full.at[t], out.at[t], out_sem.at[t])

    def one(t, carry):
        for k in range(slots):
            at = place[t * slots + k]
            value = packed[jnp.maximum(at, 0)]
            full[t, k] = jnp.where(at >= 0, value, jnp.zeros_like(value))
        leave(t).start()
        return carry

    lax.fori_loop(0, targets, one, 0)

    def drain(t, carry):
        leave(t).wait()
        return carry

    lax.fori_loop(0, targets, drain, 0)


def place_tiles(targets, slots, place, packed):
    rows, tile = packed.shape[1:]
    shape = (targets, slots, rows, tile)
    hbm = pl.BlockSpec(memory_space=pl.ANY)
    return pl.pallas_call(
        place_kernel,
        out_shape=jax.ShapeDtypeStruct(shape, packed.dtype),
        in_specs=[pl.BlockSpec(memory_space=pltpu.SMEM), pl.BlockSpec(memory_space=pltpu.VMEM)],
        out_specs=hbm,
        scratch_shapes=[
            pltpu.VMEM(shape, packed.dtype),
            DMA((targets,)),
        ],
        compiler_params=pltpu.CompilerParams(vmem_limit_bytes=32 * 2**20),
        name="place_tiles",
    )(place, packed)


def on_device(dec_rows, enc_rows, src_act, src_slots, counts, used_tiles):
    layers, used = used_tiles.shape
    group = lax.axis_size("feat") // layers
    width = lax.axis_size("width")
    targets, maxs = src_slots.shape
    tile = enc_rows.shape[0] // targets
    depth = dec_rows.shape[1]
    members = dec_rows.shape[0] // tile
    dec = dec_rows.reshape(members, tile, depth)
    enc = enc_rows.reshape(targets, tile, depth)
    act = src_act.reshape(-1, tile)
    steps = group * (targets // 2)
    slots = targets * maxs

    usual = Plan(steps, slots * 17 // 24, 0.84)
    def run(plan, number):
        return edges_of(plan, number, group, width, counts, src_slots, used_tiles, act, dec, enc)

    packed, place, any_over = run(usual, 0)

    def fits(packed, place):
        return place_tiles(targets, maxs, place, packed)

    def exceeds(packed, place):
        packed, place, _ = run(Plan(steps, slots, 0.0), 1)
        return place_tiles(targets, maxs, place, packed)

    return lax.cond(any_over[0] > 0, exceeds, fits, packed, place)


def solution(mesh):
    return jax.shard_map(
        on_device,
        mesh=mesh,
        in_specs=(P("feat", "width"), P("feat", "width"), P(), P("feat", None), P("feat"), P()),
        out_specs=P("feat", None, "width", None),
        check_vma=False,
    )
```

```python
import functools

import jax
import jax.numpy as jnp
from jax import lax
from jax.experimental import pallas as pl
from jax.experimental.pallas import tpu as pltpu
from jax.sharding import PartitionSpec as P

CHUNK = 8
TOP = 32767.0
MESH = pl.DeviceIdType.MESH
DMA = pltpu.SemaphoreType.DMA
PART = 256
RAW = 4


class Plan:
    def __init__(self, steps, wanted, share):
        self.steps = steps
        self.each = min(int(wanted * share) // steps, CHUNK)
        self.rest = -(-(wanted - self.each * steps) // CHUNK)
        self.lead = self.each * steps
        self.slots = self.lead + self.rest * CHUNK
        self.first = steps if self.each else 0
        self.groups = self.first + self.rest


def edge_kernel(
    plan, group, width,
    counts_in, slots_in, used_in, act_in, dec, enc, out, place_out, any_over_out,
    counts, slots, used_tiles, act, place, any_over,
    raw, table, targets, products, spread, sent, sent_scale, got, got_scale, done, flag, flags, item_rows, items,
    small_sem, item_sem, raw_sem, load_sem, group_send, group_recv, data_send, data_recv, scale_send, scale_recv, out_sem,
    flag_send, flag_recv,
):
    f, w = lax.axis_index("feat"), lax.axis_index("width")
    feats = flags.shape[0] + 1
    member = lax.rem(f, group)
    layer = f // group
    base = f - member
    members, tile, depth = dec.shape
    per = table.shape[0] // group
    pairs = targets.shape[0] // 2
    rows = tile // width
    parts = depth // PART

    def columns(p):
        return pl.ds(pl.multiple_of(p * PART, PART), PART)

    def raw_load(p, b):
        return pltpu.make_async_copy(dec.at[:, :, columns(p)], raw[b], raw_sem.at[b])

    def pair_load(j):
        two = pl.ds(2 * j, 2)
        return pltpu.make_async_copy(enc.at[two], targets.at[two], load_sem.at[j])

    for b in range(len(raw)):
        raw_load(b, b).start()
    small = [
        pltpu.make_async_copy(source, held, small_sem.at[i])
        for i, (source, held) in enumerate(
            ((used_in, used_tiles), (counts_in, counts), (slots_in, slots), (act_in, act))
        )
    ]
    for load in small:
        load.start()
    pair_load(0).start()

    barrier = pltpu.get_barrier_semaphore()


    def greet(o, carry):
        pl.semaphore_signal(barrier, 1, device_id=(lax.rem(f + o, feats), w), device_id_type=MESH)
        return carry

    lax.fori_loop(1, feats, greet, 0)
    for o in range(1, width):
        pl.semaphore_signal(barrier, 1, device_id=(f, lax.rem(w + o, width)), device_id_type=MESH)

    number = lax.broadcasted_iota(jnp.int32, item_rows.shape, 0) * item_rows.shape[1]
    number = number + lax.broadcasted_iota(jnp.int32, item_rows.shape, 1)
    tiles, maxs = slots.shape

    def list_target(at, carry):
        listed, following = carry
        inside = jnp.minimum(at, group * tiles - 1)
        o, t = inside // tiles, lax.rem(inside, tiles)
        source = lax.rem(member + group - o, group)
        floor = plan.each * (o * pairs + t // 2)
        live = jnp.where(at == inside, counts[t], 0)
        for k in range(maxs):
            s = slots[t, k]
            mine = jnp.logical_and(s // per == source, k < live)
            slot = jnp.maximum(following, floor)
            code = (o * per + lax.rem(s, per)) * tiles + t
            listed = jnp.where(number == jnp.where(mine, slot, -1), code, listed)
            n = t * maxs + k
            place[n] = jnp.where(mine, slot, jnp.where(at < tiles, -1, place[n]))
            following = jnp.where(mine, slot + 1, following)
        return listed, following

    to_items = pltpu.make_async_copy(item_rows, items, item_sem)

    def item(n):
        code = items[n // items.shape[1], lax.rem(n, items.shape[1])]
        return code // tiles, lax.rem(code, tiles)

    products[pl.ds(0, per), pl.ds(0, 2)] = jnp.zeros((per, 2, tile, tile), jnp.float32)
    pl.semaphore_wait(barrier, feats - 1 + width - 1)

    def group_copy(o, p):
        return pltpu.make_async_remote_copy(
            src_ref=table.at[pl.ds(0, per), :, columns(p)],
            dst_ref=table.at[pl.ds(o * per, per), :, columns(p)],
            send_sem=group_send.at[o - 1, p], recv_sem=group_recv.at[o - 1, p],
            device_id=(base + lax.rem(member + o, group), w), device_id_type=MESH,
        )

    for load in small:
        load.wait()

    rounds = parts // len(raw)
    portion = -(-group * tiles // (rounds - 1)) if rounds > 1 else 0

    def pick(several, carry, portion):
        for b in range(len(raw)):
            p = several * len(raw) + b
            raw_load(p, b).wait()
            for i in range(per):
                at = lax.rem(used_tiles[layer, member * per + i], members)
                table[i, :, columns(p)] = raw[b][at]
            for o in range(1, group):
                group_copy(o, p).start()

            @pl.when(p + len(raw) < parts)
            def _():
                raw_load(p + len(raw), b).start()

        @pl.when(several == 0)
        def _():
            pair_load(0).wait()

        for i in range(portion):
            carry = list_target(several * portion + i, carry)
        run = len(raw) * PART
        these = pl.ds(pl.multiple_of(several * run, run), run)
        left = table[pl.ds(0, per), :, these].reshape(per * tile, run)
        right = targets[pl.ds(0, 2), :, these].reshape(2 * tile, run)
        value = lax.dot_general(left, right, (((1,), (1,)), ((), ())), preferred_element_type=jnp.float32)
        products[pl.ds(0, per), 0] += value[:, :tile].reshape(per, tile, tile)
        products[pl.ds(0, per), 1] += value[:, tile:].reshape(per, tile, tile)

        if pairs > 1:
            @pl.when(several == rounds // 2)
            def _():
                pair_load(1).start()

        return carry

    listed, following = jnp.zeros(item_rows.shape, jnp.int32), jnp.int32(0)
    if portion:
        one_round = functools.partial(pick, portion=portion)
        listed, following = lax.fori_loop(0, rounds - 1, one_round, (listed, following))
    else:
        listed, following = lax.fori_loop(0, group * tiles, list_target, (listed, following))
    over = (following > plan.slots).astype(jnp.int32)
    item_rows[...] = listed
    to_items.start()
    give_place = pltpu.make_async_copy(place, place_out, small_sem.at[0])
    give_place.start()
    pick(jnp.int32(rounds - 1), None, 0)
    for j in range(2, pairs):
        pair_load(j).start()

    def share(o, g, start, count):
        peer = (f, lax.rem(w + o, width))
        span = pl.ds(start, count)
        data = pltpu.make_async_remote_copy(
            src_ref=sent.at[o - 1, span], dst_ref=got.at[o - 1, span],
            send_sem=data_send.at[o - 1, g], recv_sem=data_recv.at[o - 1, g],
            device_id=peer, device_id_type=MESH,
        )
        scale = pltpu.make_async_remote_copy(
            src_ref=sent_scale.at[o - 1, g], dst_ref=got_scale.at[o - 1, g],
            send_sem=scale_send.at[o - 1, g], recv_sem=scale_recv.at[o - 1, g],
            device_id=peer, device_id_type=MESH,
        )
        return data, scale

    def send(g, start, count):
        for r in range(count):
            n = start + r
            s, t = item(n)
            for o in range(1, width):
                peer = lax.rem(w + o, width)
                part = products[s, t, pl.ds(pl.multiple_of(peer * rows, rows), rows), :]
                peak = jnp.maximum(jnp.max(jnp.abs(part), axis=0, keepdims=True), 1e-30)
                sent[o - 1, n] = jnp.round(part * (TOP / peak)).astype(jnp.int32).astype(jnp.int16)
                sent_scale[o - 1, g, pl.ds(r, 1), :] = peak * (1.0 / TOP)
        for o in range(1, width):
            for copy in share(o, g, start, count):
                copy.start()

    def multiply(o, j):
        left = table[pl.ds(o * per, per)].reshape(per * tile, depth)
        right = targets[pl.ds(2 * j, 2)].reshape(2 * tile, depth)
        value = lax.dot_general(left, right, (((1,), (1,)), ((), ())), preferred_element_type=jnp.float32)
        products[pl.ds(o * per, per), 2 * j] = value[:, :tile].reshape(per, tile, tile)
        products[pl.ds(o * per, per), 2 * j + 1] = value[:, tile:].reshape(per, tile, tile)

    each = plan.each

    def first_step(j, carry):
        pair_load(j).wait()
        multiply(0, j)
        if each:
            send(j, j * each, each)
        return carry

    to_items.wait()
    if each:
        send(0, 0, each)
    lax.fori_loop(1, pairs, first_step, 0)

    def phase(o, carry):
        def arrive(p, carry):
            group_copy(o, p).wait_recv()
            return carry

        lax.fori_loop(0, parts, arrive, 0)

        def step(j, carry):
            multiply(o, j)
            if each:
                g = o * pairs + j
                send(g, g * each, each)
            return carry

        lax.fori_loop(0, pairs, step, 0)
        return carry

    lax.fori_loop(1, group, phase, 0)

    def rest_send(g, carry):
        send(plan.first + g, plan.lead + g * CHUNK, CHUNK)
        return carry

    lax.fori_loop(0, plan.rest, rest_send, 0)

    def flag_copy(o):
        return pltpu.make_async_remote_copy(
            src_ref=flag, dst_ref=flags.at[o - 1], send_sem=flag_send.at[o - 1], recv_sem=flag_recv.at[o - 1],
            device_id=(lax.rem(f + o, feats), w), device_id_type=MESH,
        )

    flag[...] = jnp.full(flag.shape, over, jnp.int32)

    def tell(o, carry):
        flag_copy(o).start()
        return carry

    lax.fori_loop(1, feats, tell, 0)

    for o in range(group):
        source = lax.rem(member + group - o, group)
        for i in range(per):
            line = act[pl.ds(used_tiles[layer, source * per + i], 1), :]
            spread[o * per + i] = jnp.broadcast_to(line, (tile, tile)).T

    def out_copy(g, start, count):
        span = pl.ds(start, count)
        return pltpu.make_async_copy(done.at[span], out.at[span], out_sem.at[g])

    def finish(g, start, count):
        for o in range(1, width):
            for copy in share(o, g, start, count):
                copy.wait_recv()
        here = pl.ds(pl.multiple_of(w * rows, rows), rows)
        for r in range(count):
            n = start + r
            s, t = item(n)
            total = products[s, t, here, :]
            for o in range(1, width):
                total = total + got[o - 1, n].astype(jnp.int32).astype(jnp.float32) * got_scale[o - 1, g, pl.ds(r, 1), :]
            done[n] = (total * spread[s, here, :]).astype(done.dtype)
        out_copy(g, start, count).start()

    def drain(g, start, count):
        for o in range(1, width):
            for copy in share(o, g, start, count):
                copy.wait_send()
        out_copy(g, start, count).wait()

    def lead(act_on):
        def one(g, carry):
            act_on(g, g * each, each)
            return carry

        lax.fori_loop(0, plan.first, one, 0)

    def rest(act_on, first, last):
        def one(g, carry):
            act_on(plan.first + g, plan.lead + g * CHUNK, CHUNK)
            return carry

        lax.fori_loop(first, last, one, 0)

    if plan.first:
        lead(finish)
    rest(finish, 0, plan.rest - 1)
    if plan.first:
        lead(drain)
    rest(drain, 0, plan.rest - 1)

    def group_drain(p, carry):
        for o in range(1, group):
            group_copy(o, p).wait_send()
        return carry

    lax.fori_loop(0, parts, group_drain, 0)

    def hear(o, highest):
        flag_copy(o).wait()
        return jnp.maximum(highest, flags[o - 1])

    any_over[0] = jnp.max(lax.fori_loop(1, feats, hear, flag[...]))
    give_over = pltpu.make_async_copy(any_over, any_over_out, small_sem.at[1])
    give_over.start()
    rest(finish, plan.rest - 1, plan.rest)
    give_place.wait()
    give_over.wait()
    rest(drain, plan.rest - 1, plan.rest)


def edges_of(plan, number, group, width, counts, slots, used_tiles, act, dec, enc):
    members, tile, depth = dec.shape
    used = used_tiles.shape[1]
    targets = enc.shape[0]
    rows = tile // width
    others = width - 1
    parts = depth // PART
    feats = lax.axis_size("feat")
    flag_kind = (8, 128)
    hbm = pl.BlockSpec(memory_space=pl.ANY)
    return pl.pallas_call(
        functools.partial(edge_kernel, plan, group, width),
        out_shape=[
            jax.ShapeDtypeStruct((plan.slots, rows, tile), jnp.bfloat16),
            jax.ShapeDtypeStruct((slots.shape[0] * slots.shape[1],), jnp.int32),
            jax.ShapeDtypeStruct((1,), jnp.int32),
        ],
        in_specs=[hbm] * 6,
        out_specs=[hbm] * 3,
        scratch_shapes=[
            pltpu.SMEM(counts.shape, jnp.int32),
            pltpu.SMEM(slots.shape, jnp.int32),
            pltpu.SMEM(used_tiles.shape, jnp.int32),
            pltpu.VMEM(act.shape, jnp.float32),
            pltpu.SMEM((slots.shape[0] * slots.shape[1],), jnp.int32),
            pltpu.SMEM((1,), jnp.int32),
            [pltpu.VMEM((members, tile, PART), jnp.bfloat16)] * min(RAW, parts),
            pltpu.VMEM((used, tile, depth), jnp.bfloat16),
            pltpu.VMEM((targets, tile, depth), jnp.bfloat16),
            pltpu.VMEM((used, targets, tile, tile), jnp.float32),
            pltpu.VMEM((used, tile, tile), jnp.float32),
            pltpu.VMEM((others, plan.slots, rows, tile), jnp.int16),
            pltpu.VMEM((others, plan.groups, CHUNK, tile), jnp.float32),
            pltpu.VMEM((others, plan.slots, rows, tile), jnp.int16),
            pltpu.VMEM((others, plan.groups, CHUNK, tile), jnp.float32),
            pltpu.VMEM((plan.slots, rows, tile), jnp.bfloat16),
            pltpu.VMEM(flag_kind, jnp.int32),
            pltpu.VMEM((feats - 1,) + flag_kind, jnp.int32),
            pltpu.VMEM(flag_kind, jnp.int32),
            pltpu.SMEM(flag_kind, jnp.int32),
            DMA((4,)),
            DMA,
            DMA((RAW,)),
            DMA((targets // 2,)),
            DMA((max(group - 1, 1), parts)),
            DMA((max(group - 1, 1), parts)),
            DMA((others, plan.groups)),
            DMA((others, plan.groups)),
            DMA((others, plan.groups)),
            DMA((others, plan.groups)),
            DMA((plan.groups,)),
            DMA((feats - 1,)),
            DMA((feats - 1,)),
        ],
        compiler_params=pltpu.CompilerParams(
            collective_id=number, has_side_effects=True, vmem_limit_bytes=(63 if number else 60) * 2**20
        ),
        name=f"edges_{plan.slots}",
    )(counts, slots, used_tiles, act, dec, enc)


def place_kernel(place, packed, out, full, out_sem):
    targets, slots = full.shape[:2]

    def leave(t):
        return pltpu.make_async_copy(full.at[t], out.at[t], out_sem.at[t])

    def one(t, carry):
        for k in range(slots):
            at = place[t * slots + k]
            value = packed[jnp.maximum(at, 0)]
            full[t, k] = jnp.where(at >= 0, value, jnp.zeros_like(value))
        leave(t).start()
        return carry

    lax.fori_loop(0, targets, one, 0)

    def drain(t, carry):
        leave(t).wait()
        return carry

    lax.fori_loop(0, targets, drain, 0)


def place_tiles(targets, slots, place, packed):
    rows, tile = packed.shape[1:]
    shape = (targets, slots, rows, tile)
    hbm = pl.BlockSpec(memory_space=pl.ANY)
    return pl.pallas_call(
        place_kernel,
        out_shape=jax.ShapeDtypeStruct(shape, packed.dtype),
        in_specs=[pl.BlockSpec(memory_space=pltpu.SMEM), pl.BlockSpec(memory_space=pltpu.VMEM)],
        out_specs=hbm,
        scratch_shapes=[
            pltpu.VMEM(shape, packed.dtype),
            DMA((targets,)),
        ],
        compiler_params=pltpu.CompilerParams(vmem_limit_bytes=32 * 2**20),
        name="place_tiles",
    )(place, packed)


def on_device(dec_rows, enc_rows, src_act, src_slots, counts, used_tiles):
    layers, used = used_tiles.shape
    group = lax.axis_size("feat") // layers
    width = lax.axis_size("width")
    targets, maxs = src_slots.shape
    tile = enc_rows.shape[0] // targets
    depth = dec_rows.shape[1]
    members = dec_rows.shape[0] // tile
    dec = dec_rows.reshape(members, tile, depth)
    enc = enc_rows.reshape(targets, tile, depth)
    act = src_act.reshape(-1, tile)
    steps = group * (targets // 2)
    slots = targets * maxs

    usual = Plan(steps, slots * 17 // 24, 0.84)
    def run(plan, number):
        return edges_of(plan, number, group, width, counts, src_slots, used_tiles, act, dec, enc)

    packed, place, any_over = run(usual, 0)

    def fits(packed, place):
        return place_tiles(targets, maxs, place, packed)

    def exceeds(packed, place):
        packed, place, _ = run(Plan(steps, slots, 0.0), 1)
        return place_tiles(targets, maxs, place, packed)

    return lax.cond(any_over[0] > 0, exceeds, fits, packed, place)


def solution(mesh):
    return jax.shard_map(
        on_device,
        mesh=mesh,
        in_specs=(P("feat", "width"), P("feat", "width"), P(), P("feat", None), P("feat"), P()),
        out_specs=P("feat", None, "width", None),
        check_vma=False,
    )
```

```python
import functools

import jax
import jax.numpy as jnp
from jax import lax
from jax.experimental import pallas as pl
from jax.experimental.pallas import tpu as pltpu
from jax.sharding import PartitionSpec as P

CHUNK = 8
TOP = 32600.0
MESH = pl.DeviceIdType.MESH
DMA = pltpu.SemaphoreType.DMA
PART = 256
RAW = 4


class Plan:
    def __init__(self, steps, wanted, share):
        self.steps = steps
        self.each = 0 if steps % 2 else min(int(wanted * share) // steps, CHUNK)
        self.rest = -(-(wanted - self.each * steps) // CHUNK)
        self.lead = self.each * steps
        self.slots = self.lead + self.rest * CHUNK
        self.first = steps if self.each else 0
        self.groups = self.first + self.rest
        self.paired = -(-self.first // 2)
        self.scales = self.paired + self.rest


def edge_kernel(
    plan, group, width,
    counts_in, slots_in, used_in, act_in, dec, enc, out, place_out, any_over_out,
    counts, slots, used_tiles, act, place, any_over,
    raw, table, targets, products, spread, sent, peaks, sent_scale, got, got_scale, done, flag, flags, item_rows, items,
    small_sem, item_sem, raw_sem, load_sem, group_send, group_recv, data_send, data_recv, scale_send, scale_recv, out_sem,
    flag_send, flag_recv,
):
    f, w = lax.axis_index("feat"), lax.axis_index("width")
    feats = flags.shape[0] + 1
    member = lax.rem(f, group)
    layer = f // group
    base = f - member
    members, tile, depth = dec.shape
    per = table.shape[0] // group
    pairs = targets.shape[0] // 2
    rows = tile // width
    parts = depth // PART

    def columns(p):
        return pl.ds(pl.multiple_of(p * PART, PART), PART)

    def raw_load(p, b):
        return pltpu.make_async_copy(dec.at[:, :, columns(p)], raw[b], raw_sem.at[b])

    def pair_load(j):
        two = pl.ds(2 * j, 2)
        return pltpu.make_async_copy(enc.at[two], targets.at[two], load_sem.at[j])

    for b in range(len(raw)):
        raw_load(b, b).start()
    small = [
        pltpu.make_async_copy(source, held, small_sem.at[i])
        for i, (source, held) in enumerate(
            ((used_in, used_tiles), (counts_in, counts), (slots_in, slots), (act_in, act))
        )
    ]
    for load in small:
        load.start()
    pair_load(0).start()

    barrier = pltpu.get_barrier_semaphore()


    def greet(o, carry):
        pl.semaphore_signal(barrier, 1, device_id=(lax.rem(f + o, feats), w), device_id_type=MESH)
        return carry

    lax.fori_loop(1, feats, greet, 0)
    for o in range(1, width):
        pl.semaphore_signal(barrier, 1, device_id=(f, lax.rem(w + o, width)), device_id_type=MESH)

    number = lax.broadcasted_iota(jnp.int32, item_rows.shape, 0) * item_rows.shape[1]
    number = number + lax.broadcasted_iota(jnp.int32, item_rows.shape, 1)
    tiles, maxs = slots.shape

    def list_target(at, carry):
        listed, following = carry
        inside = jnp.minimum(at, group * tiles - 1)
        o, t = inside // tiles, lax.rem(inside, tiles)
        source = lax.rem(member + group - o, group)
        floor = plan.each * (o * pairs + t // 2)
        live = jnp.where(at == inside, counts[t], 0)
        for k in range(maxs):
            s = slots[t, k]
            mine = jnp.logical_and(s // per == source, k < live)
            slot = jnp.maximum(following, floor)
            code = (o * per + lax.rem(s, per)) * tiles + t
            listed = jnp.where(number == jnp.where(mine, slot, -1), code, listed)
            n = t * maxs + k
            place[n] = jnp.where(mine, slot, jnp.where(at < tiles, -1, place[n]))
            following = jnp.where(mine, slot + 1, following)
        return listed, following

    to_items = pltpu.make_async_copy(item_rows, items, item_sem)

    def item(n):
        code = items[n // items.shape[1], lax.rem(n, items.shape[1])]
        return code // tiles, lax.rem(code, tiles)

    products[pl.ds(0, per), pl.ds(0, 2)] = jnp.zeros((per, 2, tile, tile), jnp.float32)
    pl.semaphore_wait(barrier, feats - 1 + width - 1)

    def group_copy(o, p):
        return pltpu.make_async_remote_copy(
            src_ref=table.at[pl.ds(0, per), :, columns(p)],
            dst_ref=table.at[pl.ds(o * per, per), :, columns(p)],
            send_sem=group_send.at[o - 1, p], recv_sem=group_recv.at[o - 1, p],
            device_id=(base + lax.rem(member + o, group), w), device_id_type=MESH,
        )

    for load in small:
        load.wait()

    rounds = parts // len(raw)
    portion = -(-group * tiles // (rounds - 1)) if rounds > 1 else 0

    def pick(several, carry, portion):
        for b in range(len(raw)):
            p = several * len(raw) + b
            raw_load(p, b).wait()
            for i in range(per):
                at = lax.rem(used_tiles[layer, member * per + i], members)
                table[i, :, columns(p)] = raw[b][at]
            for o in range(1, group):
                group_copy(o, p).start()

            @pl.when(p + len(raw) < parts)
            def _():
                raw_load(p + len(raw), b).start()

        @pl.when(several == 0)
        def _():
            pair_load(0).wait()

        for i in range(portion):
            carry = list_target(several * portion + i, carry)
        run = len(raw) * PART
        these = pl.ds(pl.multiple_of(several * run, run), run)
        left = table[pl.ds(0, per), :, these].reshape(per * tile, run)
        right = targets[pl.ds(0, 2), :, these].reshape(2 * tile, run)
        value = lax.dot_general(left, right, (((1,), (1,)), ((), ())), preferred_element_type=jnp.float32)
        products[pl.ds(0, per), 0] += value[:, :tile].reshape(per, tile, tile)
        products[pl.ds(0, per), 1] += value[:, tile:].reshape(per, tile, tile)

        if pairs > 1:
            @pl.when(several == rounds // 2)
            def _():
                pair_load(1).start()

        return carry

    listed, following = jnp.zeros(item_rows.shape, jnp.int32), jnp.int32(0)
    if portion:
        one_round = functools.partial(pick, portion=portion)
        listed, following = lax.fori_loop(0, rounds - 1, one_round, (listed, following))
    else:
        listed, following = lax.fori_loop(0, group * tiles, list_target, (listed, following))
    over = (following > plan.slots).astype(jnp.int32)
    item_rows[...] = listed
    to_items.start()
    give_place = pltpu.make_async_copy(place, place_out, small_sem.at[0])
    give_place.start()
    pick(jnp.int32(rounds - 1), None, 0)
    for j in range(2, pairs):
        pair_load(j).start()

    def share(o, g, start, count):
        peer = (f, lax.rem(w + o, width))
        span = pl.ds(start, count)
        data = pltpu.make_async_remote_copy(
            src_ref=sent.at[o - 1, span], dst_ref=got.at[o - 1, span],
            send_sem=data_send.at[o - 1, g], recv_sem=data_recv.at[o - 1, g],
            device_id=peer, device_id_type=MESH,
        )
        return data

    def share_scale(o, e):
        return pltpu.make_async_remote_copy(
            src_ref=sent_scale.at[o - 1, e], dst_ref=got_scale.at[o - 1, e],
            send_sem=scale_send.at[o - 1, e], recv_sem=scale_recv.at[o - 1, e],
            device_id=(f, lax.rem(w + o, width)), device_id_type=MESH,
        )

    def scale_of(g, paired):
        if not paired:
            return plan.paired + g - plan.first, 0, True
        return g // 2, lax.rem(g, 2), lax.rem(g, 2) == 1

    def when(condition):
        return (lambda act_on: act_on()) if condition is True else pl.when(condition)

    def send(g, start, count, paired):
        e, side, closes = scale_of(g, paired)
        for r in range(count):
            n = start + r
            s, t = item(n)
            for o in range(1, width):
                peer = lax.rem(w + o, width)
                part = products[s, t, pl.ds(pl.multiple_of(peer * rows, rows), rows), :]
                peak = jnp.maximum(jnp.max(jnp.abs(part), axis=0, keepdims=True), 1e-30)
                scale = (peak * (1.0 / TOP)).astype(jnp.bfloat16).astype(jnp.float32)
                sent[o - 1, n] = jnp.round(part * (1.0 / scale)).astype(jnp.int32).astype(jnp.int16)
                peaks[o - 1, pl.ds(side * CHUNK + r, 1), :] = scale
        for o in range(1, width):
            share(o, g, start, count).start()

        @when(closes)
        def _():
            for o in range(1, width):
                sent_scale[o - 1, e] = peaks[o - 1].astype(jnp.bfloat16)
                share_scale(o, e).start()

    def multiply(o, j):
        left = table[pl.ds(o * per, per)].reshape(per * tile, depth)
        right = targets[pl.ds(2 * j, 2)].reshape(2 * tile, depth)
        value = lax.dot_general(left, right, (((1,), (1,)), ((), ())), preferred_element_type=jnp.float32)
        products[pl.ds(o * per, per), 2 * j] = value[:, :tile].reshape(per, tile, tile)
        products[pl.ds(o * per, per), 2 * j + 1] = value[:, tile:].reshape(per, tile, tile)

    each = plan.each

    def first_step(j, carry):
        pair_load(j).wait()
        multiply(0, j)
        if each:
            send(j, j * each, each, True)
        return carry

    to_items.wait()
    if each:
        send(jnp.int32(0), 0, each, True)
    lax.fori_loop(1, pairs, first_step, 0)

    def phase(o, carry):
        def arrive(p, carry):
            group_copy(o, p).wait_recv()
            return carry

        lax.fori_loop(0, parts, arrive, 0)

        def step(j, carry):
            multiply(o, j)
            if each:
                g = o * pairs + j
                send(g, g * each, each, True)
            return carry

        lax.fori_loop(0, pairs, step, 0)
        return carry

    lax.fori_loop(1, group, phase, 0)

    def rest_send(g, carry):
        send(plan.first + g, plan.lead + g * CHUNK, CHUNK, False)
        return carry

    lax.fori_loop(0, plan.rest, rest_send, 0)

    def flag_copy(o):
        return pltpu.make_async_remote_copy(
            src_ref=flag, dst_ref=flags.at[o - 1], send_sem=flag_send.at[o - 1], recv_sem=flag_recv.at[o - 1],
            device_id=(lax.rem(f + o, feats), w), device_id_type=MESH,
        )

    flag[...] = jnp.full(flag.shape, over, jnp.int32)

    def tell(o, carry):
        flag_copy(o).start()
        return carry

    lax.fori_loop(1, feats, tell, 0)

    for o in range(group):
        source = lax.rem(member + group - o, group)
        for i in range(per):
            line = act[pl.ds(used_tiles[layer, source * per + i], 1), :]
            spread[o * per + i] = jnp.broadcast_to(line, (tile, tile)).T

    def out_copy(g, start, count):
        span = pl.ds(start, count)
        return pltpu.make_async_copy(done.at[span], out.at[span], out_sem.at[g])

    def finish(g, start, count, e, side):
        if side == 0:
            for o in range(1, width):
                share_scale(o, e).wait_recv()

        lines = []
        for o in range(1, width):
            share(o, g, start, count).wait_recv()
            both = got_scale[o - 1, e].astype(jnp.float32)
            lines.append(both[side * CHUNK : (side + 1) * CHUNK])
        here = pl.ds(pl.multiple_of(w * rows, rows), rows)
        for r in range(count):
            n = start + r
            s, t = item(n)
            total = products[s, t, here, :]
            for o in range(1, width):
                total = total + got[o - 1, n].astype(jnp.int32).astype(jnp.float32) * lines[o - 1][r : r + 1, :]
            done[n] = (total * spread[s, here, :]).astype(done.dtype)
        out_copy(g, start, count).start()

    def drain(g, start, count, e, side):
        if side == 0:
            for o in range(1, width):
                share_scale(o, e).wait_send()

        for o in range(1, width):
            share(o, g, start, count).wait_send()
        out_copy(g, start, count).wait()

    def lead(act_on):
        def one(e, carry):
            for side in range(2):
                g = 2 * e + side
                act_on(g, g * each, each, e, side)
            return carry

        lax.fori_loop(0, plan.paired, one, 0)

    def rest(act_on, first, last):
        def one(g, carry):
            act_on(plan.first + g, plan.lead + g * CHUNK, CHUNK, plan.paired + g, 0)
            return carry

        lax.fori_loop(first, last, one, 0)

    if plan.first:
        lead(finish)
    rest(finish, 0, plan.rest - 1)
    if plan.first:
        lead(drain)
    rest(drain, 0, plan.rest - 1)

    def group_drain(p, carry):
        for o in range(1, group):
            group_copy(o, p).wait_send()
        return carry

    lax.fori_loop(0, parts, group_drain, 0)

    def hear(o, highest):
        flag_copy(o).wait()
        return jnp.maximum(highest, flags[o - 1])

    any_over[0] = jnp.max(lax.fori_loop(1, feats, hear, flag[...]))
    give_over = pltpu.make_async_copy(any_over, any_over_out, small_sem.at[1])
    give_over.start()
    rest(finish, plan.rest - 1, plan.rest)
    give_place.wait()
    give_over.wait()
    rest(drain, plan.rest - 1, plan.rest)


def edges_of(plan, number, group, width, counts, slots, used_tiles, act, dec, enc):
    members, tile, depth = dec.shape
    used = used_tiles.shape[1]
    targets = enc.shape[0]
    rows = tile // width
    others = width - 1
    parts = depth // PART
    feats = lax.axis_size("feat")
    flag_kind = (8, 128)
    hbm = pl.BlockSpec(memory_space=pl.ANY)
    return pl.pallas_call(
        functools.partial(edge_kernel, plan, group, width),
        out_shape=[
            jax.ShapeDtypeStruct((plan.slots, rows, tile), jnp.bfloat16),
            jax.ShapeDtypeStruct((slots.shape[0] * slots.shape[1],), jnp.int32),
            jax.ShapeDtypeStruct((1,), jnp.int32),
        ],
        in_specs=[hbm] * 6,
        out_specs=[hbm] * 3,
        scratch_shapes=[
            pltpu.SMEM(counts.shape, jnp.int32),
            pltpu.SMEM(slots.shape, jnp.int32),
            pltpu.SMEM(used_tiles.shape, jnp.int32),
            pltpu.VMEM(act.shape, jnp.float32),
            pltpu.SMEM((slots.shape[0] * slots.shape[1],), jnp.int32),
            pltpu.SMEM((1,), jnp.int32),
            [pltpu.VMEM((members, tile, PART), jnp.bfloat16)] * min(RAW, parts),
            pltpu.VMEM((used, tile, depth), jnp.bfloat16),
            pltpu.VMEM((targets, tile, depth), jnp.bfloat16),
            pltpu.VMEM((used, targets, tile, tile), jnp.float32),
            pltpu.VMEM((used, tile, tile), jnp.float32),
            pltpu.VMEM((others, plan.slots, rows, tile), jnp.int16),
            pltpu.VMEM((others, 2 * CHUNK, tile), jnp.float32),
            pltpu.VMEM((others, plan.scales, 2 * CHUNK, tile), jnp.bfloat16),
            pltpu.VMEM((others, plan.slots, rows, tile), jnp.int16),
            pltpu.VMEM((others, plan.scales, 2 * CHUNK, tile), jnp.bfloat16),
            pltpu.VMEM((plan.slots, rows, tile), jnp.bfloat16),
            pltpu.VMEM(flag_kind, jnp.int32),
            pltpu.VMEM((feats - 1,) + flag_kind, jnp.int32),
            pltpu.VMEM(flag_kind, jnp.int32),
            pltpu.SMEM(flag_kind, jnp.int32),
            DMA((4,)),
            DMA,
            DMA((RAW,)),
            DMA((targets // 2,)),
            DMA((max(group - 1, 1), parts)),
            DMA((max(group - 1, 1), parts)),
            DMA((others, plan.groups)),
            DMA((others, plan.groups)),
            DMA((others, plan.scales)),
            DMA((others, plan.scales)),
            DMA((plan.groups,)),
            DMA((feats - 1,)),
            DMA((feats - 1,)),
        ],
        compiler_params=pltpu.CompilerParams(
            collective_id=number, has_side_effects=True, vmem_limit_bytes=(63 if number else 60) * 2**20
        ),
        name=f"edges_{plan.slots}",
    )(counts, slots, used_tiles, act, dec, enc)


def place_kernel(place, packed, out, full, out_sem):
    targets, slots = full.shape[:2]

    def leave(t):
        return pltpu.make_async_copy(full.at[t], out.at[t], out_sem.at[t])

    def one(t, carry):
        for k in range(slots):
            at = place[t * slots + k]
            value = packed[jnp.maximum(at, 0)]
            full[t, k] = jnp.where(at >= 0, value, jnp.zeros_like(value))
        leave(t).start()
        return carry

    lax.fori_loop(0, targets, one, 0)

    def drain(t, carry):
        leave(t).wait()
        return carry

    lax.fori_loop(0, targets, drain, 0)


def place_tiles(targets, slots, place, packed):
    rows, tile = packed.shape[1:]
    shape = (targets, slots, rows, tile)
    hbm = pl.BlockSpec(memory_space=pl.ANY)
    return pl.pallas_call(
        place_kernel,
        out_shape=jax.ShapeDtypeStruct(shape, packed.dtype),
        in_specs=[pl.BlockSpec(memory_space=pltpu.SMEM), pl.BlockSpec(memory_space=pltpu.VMEM)],
        out_specs=hbm,
        scratch_shapes=[
            pltpu.VMEM(shape, packed.dtype),
            DMA((targets,)),
        ],
        compiler_params=pltpu.CompilerParams(vmem_limit_bytes=32 * 2**20),
        name="place_tiles",
    )(place, packed)


def on_device(dec_rows, enc_rows, src_act, src_slots, counts, used_tiles):
    layers, used = used_tiles.shape
    group = lax.axis_size("feat") // layers
    width = lax.axis_size("width")
    targets, maxs = src_slots.shape
    tile = enc_rows.shape[0] // targets
    depth = dec_rows.shape[1]
    members = dec_rows.shape[0] // tile
    dec = dec_rows.reshape(members, tile, depth)
    enc = enc_rows.reshape(targets, tile, depth)
    act = src_act.reshape(-1, tile)
    steps = group * (targets // 2)
    slots = targets * maxs

    usual = Plan(steps, slots * 17 // 24, 0.84)
    def run(plan, number):
        return edges_of(plan, number, group, width, counts, src_slots, used_tiles, act, dec, enc)

    packed, place, any_over = run(usual, 0)

    def fits(packed, place):
        return place_tiles(targets, maxs, place, packed)

    def exceeds(packed, place):
        packed, place, _ = run(Plan(steps, slots, 0.0), 1)
        return place_tiles(targets, maxs, place, packed)

    return lax.cond(any_over[0] > 0, exceeds, fits, packed, place)


def solution(mesh):
    return jax.shard_map(
        on_device,
        mesh=mesh,
        in_specs=(P("feat", "width"), P("feat", "width"), P(), P("feat", None), P("feat"), P()),
        out_specs=P("feat", None, "width", None),
        check_vma=False,
    )
```
